256 devices in a mesh: sec: 4 (over x_hi, core), rows: 64 (over y, x_lo, z).
Axes of the slice: x: 4 (x_hi: 2, x_lo: 2; x = x_hi * 2 + x_lo), y: 4, z: 8, core: 2. Of those that a mesh axis runs over, the one named last changes fastest.
Arguments:
- streams: bfloat16 [4, 2, 128, 64, 256], P('sec', None, 'rows'), may hold values from -6 to 6
- cotangents: bfloat16 [4, 2, 128, 64, 256], P('sec', None, 'rows'), may hold values from -6 to 6
- weights: bfloat16 [4, 1, 2, 3, 3, 256, 256], P('sec'), may hold values from -0.125 to 0.125
Outputs:
- input_streams: bfloat16 [4, 2, 128, 64, 256], P('sec', None, 'rows')
- input_grads: bfloat16 [4, 2, 128, 64, 256], P('sec', None, 'rows')
- weight_grads: float32 [4, 4608, 256], P('sec', 'rows')
The draws below stay inside these ranges and needn't reach their ends.
All inputs are finite; a program needn't handle non-finite values.
Results may differ from the reference program's by a relative error of at most 0.019.
Values may be sent and summed in bfloat16 or wider, within the bound.
No kernel may reach another device: no remote copies, remote signals or barrier semaphores. Data moves between devices by JAX's collectives and lax.ppermute only.
A program may use at most 64 MiB of HBM per device.

```python
import jax
import jax.numpy as jnp
from jax import lax

C = 256
LAYERS = 1
WIDTH = 64
SECTIONS = 4
CROPS = 4
HEIGHT = 128
N_SEC = 4


def levels(rng, shape, pieces, low, top_value):
    factor_of, own = 1.0, jax.random.fold_in(rng, 6)
    for dim, parts in pieces:
        heights = jnp.exp(jax.random.uniform(jax.random.fold_in(own, dim), (parts,), jnp.float32, low / len(pieces), top_value / len(pieces)))
        factor_of = factor_of * jnp.repeat(heights, shape[dim] // parts).reshape([-1 if axis == dim else 1 for axis in range(len(shape))])
    return factor_of


def centred(own_key, dims, spread, bound, shards=(), kind=jnp.bfloat16):
    values = spread * jax.random.normal(own_key, dims, jnp.float32)
    if shards:
        values = values * levels(own_key, dims, shards, -0.22, 0.18)
    return jnp.clip(values, -bound, bound).astype(kind)


def setup_inputs(seed: int = 0) -> dict:
    key_of = jax.random.split(jax.random.key(seed), 4)
    streams = centred(key_of[0], (CROPS, 2, HEIGHT, WIDTH, C), 1.0, 6.0, ((0, 4), (2, 64)))
    cotangents = centred(key_of[1], (CROPS, 2, HEIGHT, WIDTH, C), 1.0, 6.0, ((0, 4), (2, 64)))
    weights = centred(key_of[2], (SECTIONS, LAYERS, 2, 3, 3, C, C), (9 * C) ** -0.5, 0.125, ((0, 4),))
    return {"streams": streams, "cotangents": cotangents, "weights": weights}


def conv_same(field, kernel):
    return lax.conv_general_dilated(field.astype(jnp.float32)[None], kernel.astype(jnp.float32), (1, 1), ((1, 1), (1, 1)), dimension_numbers=("NHWC", "HWIO", "NHWC"), precision=lax.Precision.HIGHEST)[0]


def turn_kernel(kernel):
    return jnp.flip(kernel, (0, 1)).swapaxes(2, 3)


def silu_slope(value):
    sig = jax.nn.sigmoid(value)
    return sig + value * sig * (1.0 - sig)


def tap_grads(act, cotan):
    padded = jnp.pad(act.astype(jnp.float32), ((1, 1), (1, 1), (0, 0)))
    height, width = cotan.shape[0], cotan.shape[1]
    patches = jnp.stack([padded[row_tap:row_tap + height, col_tap:col_tap + width] for row_tap in range(3) for col_tap in range(3)])
    summed = jnp.einsum("khwi,hwo->kio", patches, cotan.astype(jnp.float32), precision=lax.Precision.HIGHEST)
    return summed.reshape(3, 3, act.shape[-1], cotan.shape[-1])


def layer_back(state, kernel_f, kernel_g):
    upper = state[0].astype(jnp.float32)
    act_g = jax.nn.silu(upper).astype(jnp.bfloat16)
    lower_in = (state[1].astype(jnp.float32) - conv_same(act_g, kernel_g)).astype(jnp.bfloat16)
    carried = (state[2].astype(jnp.float32) + conv_same(state[3], turn_kernel(kernel_g)) * silu_slope(upper)).astype(jnp.bfloat16)
    grad_g = tap_grads(act_g, state[3])
    lower_wide = lower_in.astype(jnp.float32)
    act_f = jax.nn.silu(lower_wide).astype(jnp.bfloat16)
    upper_in = (upper - conv_same(act_f, kernel_f)).astype(jnp.bfloat16)
    grad_lower_in = (state[3].astype(jnp.float32) + conv_same(carried, turn_kernel(kernel_f)) * silu_slope(lower_wide)).astype(jnp.bfloat16)
    grad_f = tap_grads(act_f, carried)
    return jnp.stack([upper_in, lower_in, carried, grad_lower_in]), grad_f, grad_g


def reference(streams, cotangents, weights):
    grads = jnp.zeros((N_SEC, LAYERS, 2, 3, 3, C, C), jnp.float32)
    results = []
    for crop in range(CROPS):
        state = jnp.concatenate([streams[crop], cotangents[crop]], 0)
        for section in reversed(range(N_SEC)):
            for layer in reversed(range(LAYERS)):
                state, grad_f, grad_g = layer_back(state, weights[section, layer, 0], weights[section, layer, 1])
                grads = grads.at[section, layer, 0].add(grad_f)
                grads = grads.at[section, layer, 1].add(grad_g)
        results.append(state)
    finished = jnp.stack(results)
    scale = (CROPS * HEIGHT * WIDTH) ** -0.5
    weight_grads = (grads * scale).reshape(N_SEC, LAYERS * 18 * C, C)
    return finished[:, :2], finished[:, 2:], weight_grads
```

```python
import functools

import jax
import jax.numpy as jnp
from jax import lax
from jax.experimental import pallas as pl
from jax.experimental.pallas import tpu as pltpu
from jax.sharding import PartitionSpec as P

BF = jnp.bfloat16
F32 = jnp.float32
NX = 2
NZ = 8


VM = pl.BlockSpec(memory_space=pltpu.VMEM)
ANY = pl.BlockSpec(memory_space=pl.ANY)


def silu_slope(value, sig):
    return sig + value * sig * (1.0 - sig)


def col_shifts(value, width):
    n = value.shape[0]
    col = lax.broadcasted_iota(jnp.int32, value.shape, 0) % width
    left = jnp.where(col == 0, 0.0, pltpu.roll(value, 1, 0))
    right = jnp.where(col == width - 1, 0.0, pltpu.roll(value, n - 1, 0))
    return [left.astype(BF), value.astype(BF), right.astype(BF)]


def conv(shifts, kernel, rows, width):
    total = None
    for a in range(3):
        for b in range(3):
            term = jnp.dot(
                shifts[b][a * width : (a + rows) * width],
                kernel[a, b],
                preferred_element_type=F32,
            )
            total = term if total is None else total + term
    return total


def conv_turned(shifts, kernel, rows, width):
    total = None
    for a in range(3):
        for b in range(3):
            term = lax.dot_general(
                shifts[b][a * width : (a + rows) * width],
                kernel[2 - a, 2 - b],
                (((1,), (1,)), ((), ())),
                preferred_element_type=F32,
            )
            total = term if total is None else total + term
    return total


def section_kernel(
    width, sections_high, state_ref, a_ref, b_ref, own_ref, swap_ref, far_ref, farswap_ref,
    out_ref, senda_ref, sendb_ref, acts_ref, f_ref, g_ref, sem_f, sem_g,
):
    sec = lax.axis_index("sec")
    row = lax.axis_index("rows")
    last = lax.axis_size("rows") - 1
    half, core = sec // 2, sec % 2
    high, parity = sections_high
    even = row % 2 == 0
    w = width

    def fetch(pick_f, pick_g):
        pltpu.make_async_copy(pick_g, g_ref, sem_g).start()
        pltpu.make_async_copy(pick_f, f_ref, sem_f).start()

    near = half == high
    mine = core == parity

    @pl.when(near & mine)
    def _():
        fetch(own_ref.at[0], own_ref.at[1])

    @pl.when(near & jnp.logical_not(mine))
    def _():
        fetch(swap_ref.at[0], swap_ref.at[1])

    @pl.when(jnp.logical_not(near) & (core == 0))
    def _():
        fetch(far_ref, farswap_ref)

    @pl.when(jnp.logical_not(near) & (core == 1))
    def _():
        fetch(farswap_ref, far_ref)

    got_a, got_b = a_ref[...], b_ref[...]
    up = jnp.where(even, got_b, got_a).astype(F32)
    down = jnp.where(even, got_a, got_b).astype(F32)
    y1 = state_ref[0].astype(F32)
    y2 = state_ref[1].astype(F32)
    g1 = state_ref[2].astype(F32)
    g2 = state_ref[3].astype(F32)
    y1x = jnp.concatenate([up[: 2 * w], y1, down[: 2 * w]], 0)
    g2x = jnp.concatenate([up[2 * w : 4 * w], g2, down[2 * w : 4 * w]], 0)
    y2x = jnp.concatenate([up[4 * w : 5 * w], y2, down[4 * w : 5 * w]], 0)
    g1x = jnp.concatenate([up[5 * w :], g1, down[5 * w :]], 0)
    line = lax.broadcasted_iota(jnp.int32, (4 * w, 1), 0) // w
    inside = ((line > 0) | (row > 0)) & ((line < 3) | (row < last))

    sig1 = jax.nn.sigmoid(y1x)
    act_g = (y1x * sig1).astype(BF).astype(F32)
    shifts_g = col_shifts(act_g, w)
    shifts_c = col_shifts(g2x, w)
    pltpu.make_async_copy(own_ref.at[1], g_ref, sem_g).wait()
    x2 = y2x - conv(shifts_g, g_ref, 4, w)
    x2 = jnp.where(inside, x2, 0.0).astype(BF)
    slope1 = silu_slope(y1x, sig1)[w : 5 * w]
    carried = g1x + conv_turned(shifts_c, g_ref, 4, w) * slope1
    carried = jnp.where(inside, carried, 0.0).astype(BF)
    x2w = x2.astype(F32)
    sig2 = jax.nn.sigmoid(x2w)
    act_f = (x2w * sig2).astype(BF)
    shifts_f = col_shifts(act_f.astype(F32), w)
    shifts_d = col_shifts(carried.astype(F32), w)
    pltpu.make_async_copy(own_ref.at[0], f_ref, sem_f).wait()
    x1 = (y1 - conv(shifts_f, f_ref, 2, w)).astype(BF)
    slope2 = silu_slope(x2w, sig2)[w : 3 * w]
    gx2 = (g2 + conv_turned(shifts_d, f_ref, 2, w) * slope2).astype(BF)
    out_ref[0] = x1
    out_ref[1] = x2[w : 3 * w]
    out_ref[2] = carried[w : 3 * w]
    out_ref[3] = gx2
    for ref, low in ((senda_ref, even), (sendb_ref, jnp.logical_not(even))):
        ref[: 2 * w] = x1
        ref[2 * w : 4 * w] = gx2
        ref[4 * w : 5 * w] = jnp.where(low, x2[2 * w : 3 * w].astype(F32), x2[w : 2 * w].astype(F32)).astype(BF)
        ref[5 * w :] = jnp.where(
            low, carried[2 * w : 3 * w].astype(F32), carried[w : 2 * w].astype(F32)
        ).astype(BF)
    acts_ref[: 4 * w] = act_g[w : 5 * w].astype(BF)
    acts_ref[4 * w : 6 * w] = state_ref[3]
    acts_ref[6 * w : 10 * w] = act_f
    acts_ref[10 * w :] = carried[w : 3 * w]


def section_step(high, parity, state, got, weights):
    _, pixels, channels = state.shape
    width = pixels // 2
    shapes = (
        jax.ShapeDtypeStruct(state.shape, BF),
        jax.ShapeDtypeStruct((6 * width, channels), BF),
        jax.ShapeDtypeStruct((6 * width, channels), BF),
        jax.ShapeDtypeStruct((12 * width, channels), BF),
    )
    return pl.pallas_call(
        functools.partial(section_kernel, width, (high, parity)),
        out_shape=shapes,
        in_specs=[VM] * 3 + [ANY] * 4,
        out_specs=[VM] * 4,
        scratch_shapes=[
            pltpu.VMEM((3, 3, channels, channels), BF),
            pltpu.VMEM((3, 3, channels, channels), BF),
            pltpu.SemaphoreType.DMA,
            pltpu.SemaphoreType.DMA,
        ],
        cost_estimate=pl.CostEstimate(
            flops=48 * 9 * width * channels * channels, bytes_accessed=4 << 20, transcendentals=0
        ),
        name="section_step",
    )(state, *got, *weights)


def pack_kernel(width, state_ref, senda_ref, sendb_ref):
    even = lax.axis_index("rows") % 2 == 0
    w = width
    for ref, low in ((senda_ref, even), (sendb_ref, jnp.logical_not(even))):
        ref[: 2 * w] = state_ref[0]
        ref[2 * w : 4 * w] = state_ref[3]
        for place, part in ((4, 1), (5, 2)):
            both = state_ref[part].astype(F32)
            ref[place * w : (place + 1) * w] = jnp.where(low, both[w:], both[:w]).astype(BF)


def pack(state):
    _, pixels, channels = state.shape
    width = pixels // 2
    shape = jax.ShapeDtypeStruct((6 * width, channels), BF)
    return pl.pallas_call(
        functools.partial(pack_kernel, width),
        out_shape=(shape, shape),
        in_specs=[VM],
        out_specs=[VM, VM],
        name="pack_edges",
    )(state)


def grads_kernel(width, ny, a0, a1, a2, a3, keep_ref, send_ref, acc_ref):
    w = width
    channels = a0.shape[-1]
    y = lax.axis_index("rows") // (NX * NZ)
    for kernel, (act_at, cot_at) in enumerate(((6, 10), (0, 4))):
        shifts = []
        for ref in (a0, a1, a2, a3):
            shifts.append(col_shifts(ref[act_at * w : (act_at + 4) * w].astype(F32), w))
        cot = jnp.concatenate([ref[cot_at * w : (cot_at + 2) * w] for ref in (a0, a1, a2, a3)], 0)
        for a in range(3):
            for b in range(3):
                act = jnp.concatenate([s[b][a * w : (a + 2) * w] for s in shifts], 0)
                at = ((kernel * 3 + a) * 3 + b) * channels
                acc_ref[at : at + channels] = lax.dot_general(
                    act, cot, (((0,), (0,)), ((), ())), preferred_element_type=F32
                )
    size = 18 * channels // ny
    keep_ref[...] = acc_ref[pl.ds(pl.multiple_of(y * size, 8), size)]
    for k in range(1, ny):
        at = pl.multiple_of(lax.rem(y + k, ny) * size, 8)
        send_ref[k - 1] = acc_ref[pl.ds(at, size)].astype(BF)


def section_grads(acts, ny, width):
    channels = acts[0].shape[-1]
    size = 18 * channels // ny
    return pl.pallas_call(
        functools.partial(grads_kernel, width, ny),
        out_shape=(
            jax.ShapeDtypeStruct((size, channels), F32),
            jax.ShapeDtypeStruct((ny - 1, size, channels), BF),
        ),
        in_specs=[VM] * 4,
        out_specs=[VM, VM],
        scratch_shapes=[pltpu.VMEM((18 * channels, channels), F32)],
        name="section_grads",
    )(*acts)


def add_kernel(keep_ref, *refs):
    total = keep_ref[...]
    for ref in refs[:-1]:
        total = total + ref[...].astype(F32)
    refs[-1][...] = total.astype(BF)


def add_up(keep, terms):
    return pl.pallas_call(
        add_kernel,
        out_shape=jax.ShapeDtypeStruct(keep.shape, BF),
        in_specs=[VM] * (1 + len(terms)),
        out_specs=VM,
        name="add_terms",
    )(keep, *terms)


def local(streams, cotangents, weights):
    rows = lax.axis_size("rows")
    ny = rows // (NX * NZ)
    crops, _, height_dev, width, channels = streams.shape
    core = lax.axis_index("sec") % 2
    scale = float(4 * height_dev * rows * width) ** -0.5

    swap_pairs = [(s, s ^ 1) for s in range(4)]
    cross_pairs = []
    for sec in range(4):
        for r in range(rows):
            cross_pairs.append((sec * rows + r, (sec ^ 2) * rows + (r ^ NZ)))
    pairs_a = [(r, r ^ 1) for r in range(rows)]
    pairs_b = [p for r in range(1, rows - 1, 2) for p in ((r, r + 1), (r + 1, r))]

    def core_swap(value):
        return lax.ppermute(value, "sec", swap_pairs)

    def cross(value):
        return lax.ppermute(value, ("sec", "rows"), cross_pairs)

    def halo(sends):
        return lax.ppermute(sends[0], "rows", pairs_a), lax.ppermute(sends[1], "rows", pairs_b)

    own = weights[0, 0]
    swapped = core_swap(own)
    first = core == 0
    odd_piece = jnp.where(first, swapped[0], own[1])
    even_piece = jnp.where(first, own[0], swapped[1])
    state = jnp.concatenate([streams[0], cotangents[0]], 0).reshape(4, height_dev * width, channels)
    got = halo(pack(state))
    far_odd = cross(odd_piece)
    farswap_odd = core_swap(far_odd)
    far_even = cross(even_piece)
    farswap_even = core_swap(far_even)

    odd = (own, swapped, far_odd, farswap_odd)
    even = (own, swapped, far_even, farswap_even)
    acts = {}
    for section in (3, 2, 1, 0):
        state, *sends, acts[section] = section_step(
            section // 2, section % 2, state, got, odd if section % 2 else even
        )
        if section:
            got = halo(sends)

    sec = lax.axis_index("sec")
    stacked = jnp.stack([acts[s] for s in range(4)])
    mine = [lax.dynamic_index_in_dim(stacked, sec, 0, False)]
    for k in (1, 2, 3):
        mine.append(
            lax.ppermute(
                lax.dynamic_index_in_dim(stacked, sec ^ k, 0, False),
                "sec",
                [(s, s ^ k) for s in range(4)],
            )
        )
    keep, sends = section_grads(mine, ny, width)
    terms = []
    for k in range(1, ny):
        pairs = [(r, (r + k * NX * NZ) % rows) for r in range(rows)]
        terms.append(lax.ppermute(sends[k - 1], "rows", pairs))
    total = add_up(keep, terms).reshape(NX * NZ, -1, channels)
    groups = [[y * NX * NZ + q for q in range(NX * NZ)] for y in range(ny)]
    parts = lax.all_to_all(total, "rows", 0, 0, axis_index_groups=groups)
    shard = jnp.sum(parts.astype(F32), 0) * scale
    result = state.reshape(1, 4, height_dev, width, channels)
    return result[:, :2], result[:, 2:], shard[None]


def solution(mesh):
    placed = (
        P("sec", None, "rows", None, None),
        P("sec", None, "rows", None, None),
        P("sec", None, None, None, None, None, None),
    )
    return jax.shard_map(
        local,
        mesh=mesh,
        in_specs=placed,
        out_specs=(
            P("sec", None, "rows", None, None),
            P("sec", None, "rows", None, None),
            P("sec", "rows", None),
        ),
        check_vma=False,
    )
```

```python
import functools

import jax
import jax.numpy as jnp
from jax import lax
from jax.experimental import pallas as pl
from jax.experimental.pallas import tpu as pltpu
from jax.sharding import PartitionSpec as P

BF = jnp.bfloat16
F32 = jnp.float32
NX = 2
NZ = 8
GRANT = 24 << 20


VM = pl.BlockSpec(memory_space=pltpu.VMEM)
ANY = pl.BlockSpec(memory_space=pl.ANY)


barrier = lax.optimization_barrier


def silu_slope(value, sig):
    return sig + value * sig * (1.0 - sig)


def col_shifts(value, width):
    n = value.shape[0]
    col = lax.broadcasted_iota(jnp.int32, value.shape, 0) % width
    left = jnp.where(col == 0, 0.0, pltpu.roll(value, 1, 0))
    right = jnp.where(col == width - 1, 0.0, pltpu.roll(value, n - 1, 0))
    return [left.astype(BF), value.astype(BF), right.astype(BF)]


def tap(a, b, kernel):
    size = kernel.shape[1]
    at = (a * 3 + b) * size
    return slice(at, at + size)


def conv(shifts, kernel, rows, width):
    total = None
    for a in range(3):
        for b in range(3):
            term = jnp.dot(
                shifts[b][a * width : (a + rows) * width],
                kernel[tap(a, b, kernel)],
                preferred_element_type=F32,
            )
            total = term if total is None else total + term
    return total


def conv_turned(shifts, kernel, rows, width):
    total = None
    for a in range(3):
        for b in range(3):
            term = lax.dot_general(
                shifts[b][a * width : (a + rows) * width],
                kernel[tap(2 - a, 2 - b, kernel)],
                (((1,), (1,)), ((), ())),
                preferred_element_type=F32,
            )
            total = term if total is None else total + term
    return total


def quarter_of(row):
    x, y, z = row // NZ % NX, row // (NX * NZ) % 2, row % 2
    return x ^ (2 * y) ^ (3 * z)


def section_kernel(
    width, high, parity, top_ref, low_ref, a_ref, b_ref, own_ref, swap_ref,
    m0, m1, m2, m3, s0, s1, s2, s3,
    out_top, out_low, senda_ref, sendb_ref, acts_ref, f_ref, g_ref, sem_f, sem_g,
):
    sec = lax.axis_index("sec")
    row = lax.axis_index("rows")
    last = lax.axis_size("rows") - 1
    half, core = sec // 2, sec % 2
    even = row % 2 == 0
    w = width
    size = m0.shape[0]
    quarter = quarter_of(row)
    near = half == high
    mine = core == parity

    def whole(ref):
        pltpu.make_async_copy(ref.at[1], g_ref, sem_g).start()
        pltpu.make_async_copy(ref.at[0], f_ref, sem_f).start()

    def pieces(quarters, out, sem):
        for j, ref in enumerate(quarters):
            at = pl.multiple_of((quarter ^ j) * size, 16)
            pltpu.make_async_copy(ref, out.at[pl.ds(at, size)], sem).start()

    @pl.when(near & mine)
    def _():
        whole(own_ref)

    @pl.when(near & jnp.logical_not(mine))
    def _():
        whole(swap_ref)

    @pl.when(jnp.logical_not(near) & (core == 0))
    def _():
        pieces((s0, s1, s2, s3), g_ref, sem_g)
        pieces((m0, m1, m2, m3), f_ref, sem_f)

    @pl.when(jnp.logical_not(near) & (core == 1))
    def _():
        pieces((m0, m1, m2, m3), g_ref, sem_g)
        pieces((s0, s1, s2, s3), f_ref, sem_f)

    got_a, got_b = a_ref[...], b_ref[...]
    up = jnp.where(even, got_b, got_a).astype(F32)
    down = jnp.where(even, got_a, got_b).astype(F32)
    y1 = top_ref[0].astype(F32)
    y2 = top_ref[1].astype(F32)
    g1 = low_ref[0].astype(F32)
    g2 = low_ref[1].astype(F32)
    y1x = jnp.concatenate([up[: 2 * w], y1, down[: 2 * w]], 0)
    g2x = jnp.concatenate([up[2 * w : 4 * w], g2, down[2 * w : 4 * w]], 0)
    y2x = jnp.concatenate([up[4 * w : 5 * w], y2, down[4 * w : 5 * w]], 0)
    g1x = jnp.concatenate([up[5 * w :], g1, down[5 * w :]], 0)
    line = lax.broadcasted_iota(jnp.int32, (4 * w, 1), 0) // w
    inside = ((line > 0) | (row > 0)) & ((line < 3) | (row < last))

    sig1 = jax.nn.sigmoid(y1x)
    act_g = (y1x * sig1).astype(BF).astype(F32)
    shifts_g = col_shifts(act_g, w)
    shifts_c = col_shifts(g2x, w)
    pltpu.make_async_copy(own_ref.at[1], g_ref, sem_g).wait()
    x2 = y2x - conv(shifts_g, g_ref, 4, w)
    x2 = jnp.where(inside, x2, 0.0).astype(BF)
    slope1 = silu_slope(y1x, sig1)[w : 5 * w]
    carried = g1x + conv_turned(shifts_c, g_ref, 4, w) * slope1
    carried = jnp.where(inside, carried, 0.0).astype(BF)
    x2w = x2.astype(F32)
    sig2 = jax.nn.sigmoid(x2w)
    act_f = (x2w * sig2).astype(BF)
    shifts_f = col_shifts(act_f.astype(F32), w)
    shifts_d = col_shifts(carried.astype(F32), w)
    pltpu.make_async_copy(own_ref.at[0], f_ref, sem_f).wait()
    x1 = (y1 - conv(shifts_f, f_ref, 2, w)).astype(BF)
    slope2 = silu_slope(x2w, sig2)[w : 3 * w]
    gx2 = (g2 + conv_turned(shifts_d, f_ref, 2, w) * slope2).astype(BF)
    out_top[0] = x1
    out_top[1] = x2[w : 3 * w]
    out_low[0] = carried[w : 3 * w]
    out_low[1] = gx2
    for ref, low in ((senda_ref, even), (sendb_ref, jnp.logical_not(even))):
        ref[: 2 * w] = x1
        ref[2 * w : 4 * w] = gx2
        ref[4 * w : 5 * w] = jnp.where(low, x2[2 * w : 3 * w].astype(F32), x2[w : 2 * w].astype(F32)).astype(BF)
        ref[5 * w :] = jnp.where(
            low, carried[2 * w : 3 * w].astype(F32), carried[w : 2 * w].astype(F32)
        ).astype(BF)
    acts_ref[: 4 * w] = act_g[w : 5 * w].astype(BF)
    acts_ref[4 * w : 6 * w] = low_ref[1]
    acts_ref[6 * w : 10 * w] = act_f
    acts_ref[10 * w :] = carried[w : 3 * w]


def section_step(high, parity, state, got, weights):
    _, pixels, channels = state[0].shape
    width = pixels // 2
    shapes = (
        jax.ShapeDtypeStruct(state[0].shape, BF),
        jax.ShapeDtypeStruct(state[0].shape, BF),
        jax.ShapeDtypeStruct((6 * width, channels), BF),
        jax.ShapeDtypeStruct((6 * width, channels), BF),
        jax.ShapeDtypeStruct((12 * width, channels), BF),
    )
    return pl.pallas_call(
        functools.partial(section_kernel, width, high, parity),
        out_shape=shapes,
        in_specs=[VM] * 4 + [ANY] * 10,
        out_specs=[VM] * 5,
        scratch_shapes=[
            pltpu.VMEM((9 * channels, channels), BF),
            pltpu.VMEM((9 * channels, channels), BF),
            pltpu.SemaphoreType.DMA,
            pltpu.SemaphoreType.DMA,
        ],
        compiler_params=pltpu.CompilerParams(vmem_limit_bytes=GRANT),
        cost_estimate=pl.CostEstimate(
            flops=48 * 9 * width * channels * channels, bytes_accessed=4 << 20, transcendentals=0
        ),
        name="section_step",
    )(*state, *got, *weights)


def prepare_kernel(width, top_ref, low_ref, own_ref, senda_ref, sendb_ref, early_ref, pick_ref, sem):
    row = lax.axis_index("rows")
    even = row % 2 == 0
    core = lax.axis_index("sec") % 2
    quarter = quarter_of(row) ^ 1
    copies = [
        pltpu.make_async_copy(own_ref.at[1 - core, quarter], early_ref, sem.at[0]),
        pltpu.make_async_copy(own_ref.at[core, quarter], pick_ref, sem.at[1]),
    ]
    for copy in copies:
        copy.start()
    w = width
    for ref, low in ((senda_ref, even), (sendb_ref, jnp.logical_not(even))):
        ref[: 2 * w] = top_ref[0]
        ref[2 * w : 4 * w] = low_ref[1]
        for place, both_ref in ((4, top_ref.at[1]), (5, low_ref.at[0])):
            both = both_ref[...].astype(F32)
            ref[place * w : (place + 1) * w] = jnp.where(low, both[w:], both[:w]).astype(BF)
    for copy in copies:
        copy.wait()


def prepare(state, halves):
    _, pixels, channels = state[0].shape
    width = pixels // 2
    edge = jax.ShapeDtypeStruct((6 * width, channels), BF)
    piece = jax.ShapeDtypeStruct(halves.shape[2:], BF)
    return pl.pallas_call(
        functools.partial(prepare_kernel, width),
        out_shape=(edge, edge, piece, piece),
        in_specs=[VM, VM, ANY],
        out_specs=[VM] * 4,
        scratch_shapes=[pltpu.SemaphoreType.DMA((2,))],
        compiler_params=pltpu.CompilerParams(vmem_limit_bytes=GRANT),
        name="prepare",
    )(*state, halves)


def grads_kernel(width, sources, *refs):
    ins, (keepa, senda, keepb, sendb, a0, a1, a2, a3, acc_ref, sem) = refs[:13], refs[13:]
    w = width
    channels = a0.shape[-1]
    sec = lax.axis_index("sec")
    for section, picks in sources.items():

        @pl.when(sec == section)
        def _(picks=picks):
            for out, pick in zip((a0, a1, a2, a3), picks):
                pltpu.make_async_copy(ins[pick], out, sem).start()

    for out in (a0, a1, a2, a3):
        pltpu.make_async_copy(ins[0], out, sem).wait()
    row = lax.axis_index("rows")
    ylow, x = row // (NX * NZ) % 2, row // NZ % NX
    for kernel, (act_at, cot_at) in enumerate(((6, 10), (0, 4))):
        shifts = []
        for ref in (a0, a1, a2, a3):
            shifts.append(col_shifts(ref[act_at * w : (act_at + 4) * w].astype(F32), w))
        cot = jnp.concatenate([ref[cot_at * w : (cot_at + 2) * w] for ref in (a0, a1, a2, a3)], 0)
        for a in range(3):
            for b in range(3):
                act = jnp.concatenate([s[b][a * w : (a + 2) * w] for s in shifts], 0)
                at = ((kernel * 3 + a) * 3 + b) * channels
                acc_ref[at : at + channels] = lax.dot_general(
                    act, cot, (((0,), (0,)), ((), ())), preferred_element_type=F32
                )
    size = 18 * channels // 8
    cols = channels // 2

    def region(yhigh, ylow, x):
        return pl.ds(pl.multiple_of(((yhigh * 2 + ylow) * 2 + x) * size, 8), size)

    for i in range(2):
        for j in range(2):
            keepa[i, j] = acc_ref[region(i, j, x), :cols]
            senda[i, j] = acc_ref[region(i, j, 1 - x), :cols].astype(BF)
            keepb[i, j] = acc_ref[region(i, ylow, j), cols:]
            sendb[i, j] = acc_ref[region(i, 1 - ylow, j), cols:].astype(BF)


def section_grads(arrays, sources, width):
    channels = arrays[0].shape[-1]
    shape = (2, 2, 18 * channels // 8, channels // 2)
    return pl.pallas_call(
        functools.partial(grads_kernel, width, sources),
        out_shape=tuple(jax.ShapeDtypeStruct(shape, kind) for kind in (F32, BF, F32, BF)),
        in_specs=[ANY] * 13,
        out_specs=[VM] * 4,
        scratch_shapes=[pltpu.VMEM(arrays[0].shape, BF)] * 4
        + [pltpu.VMEM((18 * channels, channels), F32), pltpu.SemaphoreType.DMA],
        compiler_params=pltpu.CompilerParams(vmem_limit_bytes=GRANT),
        name="section_grads",
    )(*arrays)


def halve_kernel(keepa, gota, keepb, gotb, keepa2, senda2, keepb2, sendb2):
    row = lax.axis_index("rows")
    ylow, x = row // (NX * NZ) % 2, row // NZ % NX
    for keep, got, keep2, send2, bit in ((keepa, gota, keepa2, senda2, ylow), (keepb, gotb, keepb2, sendb2, x)):
        for i in range(2):
            keep2[i] = keep[i, bit] + got[i, bit].astype(F32)
            send2[i] = (keep[i, 1 - bit] + got[i, 1 - bit].astype(F32)).astype(BF)


def halve(keepa, gota, keepb, gotb):
    shape = keepa.shape[:1] + keepa.shape[2:]
    return pl.pallas_call(
        halve_kernel,
        out_shape=tuple(jax.ShapeDtypeStruct(shape, kind) for kind in (F32, BF, F32, BF)),
        in_specs=[VM] * 4,
        out_specs=[VM] * 4,
        compiler_params=pltpu.CompilerParams(vmem_limit_bytes=GRANT),
        name="halve_terms",
    )(keepa, gota, keepb, gotb)


def join_kernel(keepa, gota, keepb, gotb, out):
    cols = keepa.shape[-1]
    out[:, :, :cols] = (keepa[...] + gota[...].astype(F32)).astype(BF)
    out[:, :, cols:] = (keepb[...] + gotb[...].astype(F32)).astype(BF)


def join(keepa, gota, keepb, gotb):
    shape = keepa.shape[:-1] + (2 * keepa.shape[-1],)
    return pl.pallas_call(
        join_kernel,
        out_shape=jax.ShapeDtypeStruct(shape, BF),
        in_specs=[VM] * 4,
        out_specs=VM,
        compiler_params=pltpu.CompilerParams(vmem_limit_bytes=GRANT),
        name="join_terms",
    )(keepa, gota, keepb, gotb)


def local(streams, cotangents, weights):
    rows = lax.axis_size("rows")
    ny = rows // (NX * NZ)
    crops, _, height_dev, width, channels = streams.shape
    sec = lax.axis_index("sec")
    core = sec % 2
    first = core == 0
    scale = float(4 * height_dev * rows * width) ** -0.5

    cross_pairs = []
    for s in range(4):
        for r in range(rows):
            cross_pairs.append((s * rows + r, (s ^ 2) * rows + (r ^ NZ)))
    pairs_a = [(r, r ^ 1) for r in range(rows)]
    pairs_b = [p for r in range(1, rows - 1, 2) for p in ((r, r + 1), (r + 1, r))]

    def core_swap(value):
        return lax.ppermute(value, "sec", [(s, s ^ 1) for s in range(4)])

    def cross(value):
        return lax.ppermute(value, ("sec", "rows"), cross_pairs)

    def flip(value, bit):
        return lax.ppermute(value, "rows", [(r, r ^ bit) for r in range(rows)])

    def halo(sends):
        return lax.ppermute(sends[0], "rows", pairs_a), lax.ppermute(sends[1], "rows", pairs_b)

    own = weights[0, 0].reshape(2, 9 * channels, channels)
    state = [part.reshape(2, height_dev * width, channels) for part in (streams, cotangents)]
    *sends, early, pick = prepare(state, own.reshape(2, 4, 9 * channels // 4, channels))
    early = core_swap(early)
    odd = cross(jnp.where(first, early, pick))
    got = halo(sends)
    swapped = core_swap(own)
    odd, swapped, even, *got = barrier((odd, swapped, jnp.where(first, pick, early), *got))
    bits = (NZ, NX * NZ, 1)
    odds = [odd] + [flip(odd, bit) for bit in bits]
    even = cross(even)
    even, *odds = barrier((even, *odds))
    evens = [even] + [flip(even, bit) for bit in bits]
    far = {1: (*odds, *map(core_swap, odds))}
    acts = {}
    moved = {}
    for section in (3, 2, 1, 0):
        parity = section % 2
        *state, senda, sendb, acts[section] = section_step(
            section // 2, parity, state, got, (own, swapped) + far[parity]
        )
        if section:
            got = halo((senda, sendb))
        if section == 3:
            state[0], *evens = barrier((state[0], *evens))
            far[0] = (*evens, *map(core_swap, evens))
        if section == 1:
            moved[2], *got = barrier((moved[2], *got))
        if section == 2:
            straight = jnp.where(first, acts[2], acts[3])
            crossed = jnp.where(first, acts[3], acts[2])
            moved[2] = (
                lax.ppermute(crossed, "sec", [(2, 3), (3, 2)]),
                lax.ppermute(straight, "sec", [(0, 2), (1, 3)]),
                lax.ppermute(crossed, "sec", [(0, 3), (1, 2)]),
            )
        elif section < 2:
            moved[section] = tuple(
                lax.ppermute(acts[section], "sec", [(section ^ k, section)]) for k in (1, 2, 3)
            )

    arrays = [acts[s] for s in range(4)] + [*moved[0], *moved[1], *moved[2]]
    sources = {0: (0, 4, 5, 6), 1: (1, 7, 8, 9), 2: (2, 10, 11, 12), 3: (3, 10, 11, 12)}
    keepa, senda, keepb, sendb = section_grads(arrays, sources, width)
    gota, gotb = flip(senda, NZ), flip(sendb, NX * NZ)
    keepa, senda, keepb, sendb = halve(keepa, gota, keepb, gotb)
    gota, gotb = flip(senda, NX * NZ), flip(sendb, NZ)
    total = join(keepa, gota, keepb, gotb).reshape(2 * NZ, -1, channels)
    groups = [
        [((yhigh * 2 + ylow) * NX + x) * NZ + z for yhigh in range(ny // 2) for z in range(NZ)]
        for ylow in range(2)
        for x in range(NX)
    ]
    parts = lax.all_to_all(total, "rows", 0, 0, axis_index_groups=groups)
    shard = jnp.sum(parts.astype(F32), 0) * scale
    result = [part.reshape(1, 2, height_dev, width, channels) for part in state]
    return *result, shard[None]


def solution(mesh):
    placed = (
        P("sec", None, "rows", None, None),
        P("sec", None, "rows", None, None),
        P("sec", None, None, None, None, None, None),
    )
    return jax.shard_map(
        local,
        mesh=mesh,
        in_specs=placed,
        out_specs=(
            P("sec", None, "rows", None, None),
            P("sec", None, "rows", None, None),
            P("sec", "rows", None),
        ),
        check_vma=False,
    )
```

```python
import functools

import jax
import jax.numpy as jnp
from jax import lax
from jax.experimental import pallas as pl
from jax.experimental.pallas import tpu as pltpu
from jax.sharding import PartitionSpec as P

BF = jnp.bfloat16
F32 = jnp.float32
NX = 2
NZ = 8
GRANT = 24 << 20


VM = pl.BlockSpec(memory_space=pltpu.VMEM)
ANY = pl.BlockSpec(memory_space=pl.ANY)


barrier = lax.optimization_barrier


def silu_slope(value, sig):
    return sig + value * sig * (1.0 - sig)


def col_shifts(value, width):
    n = value.shape[0]
    col = lax.broadcasted_iota(jnp.int32, value.shape, 0) % width
    left = jnp.where(col == 0, 0.0, pltpu.roll(value, 1, 0))
    right = jnp.where(col == width - 1, 0.0, pltpu.roll(value, n - 1, 0))
    return [left.astype(BF), value.astype(BF), right.astype(BF)]


def tap(a, b, kernel):
    size = kernel.shape[1]
    at = (a * 3 + b) * size
    return slice(at, at + size)


def conv(shifts, kernel, rows, width):
    total = None
    for a in range(3):
        for b in range(3):
            term = jnp.dot(
                shifts[b][a * width : (a + rows) * width],
                kernel[tap(a, b, kernel)],
                preferred_element_type=F32,
            )
            total = term if total is None else total + term
    return total


def conv_turned(shifts, kernel, rows, width):
    total = None
    for a in range(3):
        for b in range(3):
            term = lax.dot_general(
                shifts[b][a * width : (a + rows) * width],
                kernel[tap(2 - a, 2 - b, kernel)],
                (((1,), (1,)), ((), ())),
                preferred_element_type=F32,
            )
            total = term if total is None else total + term
    return total


def quarter_of(row):
    x, y, z = row // NZ % NX, row // (NX * NZ) % 2, row % 2
    return x ^ (2 * y) ^ (3 * z)


def section_kernel(
    width, high, parity, top_ref, low_ref, a_ref, b_ref, own_ref, swap_ref,
    m0, m1, m2, m3, s0, s1, s2, s3, *refs,
):
    *older, out_top, out_low, senda_ref, sendb_ref = refs[: 4 + (len(refs) - 9) // 2]
    *acts_refs, f_ref, g_ref, sem_f, sem_g = refs[len(older) + 4 :]
    sec = lax.axis_index("sec")
    row = lax.axis_index("rows")
    last = lax.axis_size("rows") - 1
    half, core = sec // 2, sec % 2
    even = row % 2 == 0
    w = width
    size = m0.shape[0]
    quarter = quarter_of(row)
    near = half == high
    mine = core == parity

    def whole(ref):
        pltpu.make_async_copy(ref.at[1], g_ref, sem_g).start()
        pltpu.make_async_copy(ref.at[0], f_ref, sem_f).start()

    def pieces(quarters, out, sem):
        for j, ref in enumerate(quarters):
            at = pl.multiple_of((quarter ^ j) * size, 16)
            pltpu.make_async_copy(ref, out.at[pl.ds(at, size)], sem).start()

    @pl.when(near & mine)
    def _():
        whole(own_ref)

    @pl.when(near & jnp.logical_not(mine))
    def _():
        whole(swap_ref)

    @pl.when(jnp.logical_not(near) & (core == 0))
    def _():
        pieces((s0, s1, s2, s3), g_ref, sem_g)
        pieces((m0, m1, m2, m3), f_ref, sem_f)

    @pl.when(jnp.logical_not(near) & (core == 1))
    def _():
        pieces((m0, m1, m2, m3), g_ref, sem_g)
        pieces((s0, s1, s2, s3), f_ref, sem_f)

    got_a, got_b = a_ref[...], b_ref[...]
    up = jnp.where(even, got_b, got_a).astype(F32)
    down = jnp.where(even, got_a, got_b).astype(F32)
    y1 = top_ref[0].astype(F32)
    y2 = top_ref[1].astype(F32)
    g1 = low_ref[0].astype(F32)
    g2 = low_ref[1].astype(F32)
    y1x = jnp.concatenate([up[: 2 * w], y1, down[: 2 * w]], 0)
    g2x = jnp.concatenate([up[2 * w : 4 * w], g2, down[2 * w : 4 * w]], 0)
    y2x = jnp.concatenate([up[4 * w : 5 * w], y2, down[4 * w : 5 * w]], 0)
    g1x = jnp.concatenate([up[5 * w :], g1, down[5 * w :]], 0)
    line = lax.broadcasted_iota(jnp.int32, (4 * w, 1), 0) // w
    inside = ((line > 0) | (row > 0)) & ((line < 3) | (row < last))

    sig1 = jax.nn.sigmoid(y1x)
    act_g = (y1x * sig1).astype(BF).astype(F32)
    shifts_g = col_shifts(act_g, w)
    shifts_c = col_shifts(g2x, w)
    pltpu.make_async_copy(own_ref.at[1], g_ref, sem_g).wait()
    x2 = y2x - conv(shifts_g, g_ref, 4, w)
    x2 = jnp.where(inside, x2, 0.0).astype(BF)
    slope1 = silu_slope(y1x, sig1)[w : 5 * w]
    carried = g1x + conv_turned(shifts_c, g_ref, 4, w) * slope1
    carried = jnp.where(inside, carried, 0.0).astype(BF)
    x2w = x2.astype(F32)
    sig2 = jax.nn.sigmoid(x2w)
    act_f = (x2w * sig2).astype(BF)
    shifts_f = col_shifts(act_f.astype(F32), w)
    shifts_d = col_shifts(carried.astype(F32), w)
    pltpu.make_async_copy(own_ref.at[0], f_ref, sem_f).wait()
    x1 = (y1 - conv(shifts_f, f_ref, 2, w)).astype(BF)
    slope2 = silu_slope(x2w, sig2)[w : 3 * w]
    gx2 = (g2 + conv_turned(shifts_d, f_ref, 2, w) * slope2).astype(BF)
    out_top[0] = x1
    out_top[1] = x2[w : 3 * w]
    out_low[0] = carried[w : 3 * w]
    out_low[1] = gx2
    for ref, low in ((senda_ref, even), (sendb_ref, jnp.logical_not(even))):
        ref[: 2 * w] = x1
        ref[2 * w : 4 * w] = gx2
        ref[4 * w : 5 * w] = jnp.where(low, x2[2 * w : 3 * w].astype(F32), x2[w : 2 * w].astype(F32)).astype(BF)
        ref[5 * w :] = jnp.where(
            low, carried[2 * w : 3 * w].astype(F32), carried[w : 2 * w].astype(F32)
        ).astype(BF)

    def keep(ref):
        ref[: 4 * w] = act_g[w : 5 * w].astype(BF)
        ref[4 * w : 6 * w] = low_ref[1]
        ref[6 * w : 10 * w] = act_f
        ref[10 * w :] = carried[w : 3 * w]

    if older:
        stay_ref, go_ref = acts_refs

        @pl.when(half == 0)
        def _():
            keep(stay_ref)
            go_ref[...] = older[0][...]

        @pl.when(half == 1)
        def _():
            keep(go_ref)
            stay_ref[...] = older[0][...]

    else:
        keep(acts_refs[0])


def section_step(high, parity, state, got, weights, older):
    _, pixels, channels = state[0].shape
    width = pixels // 2
    shapes = (
        jax.ShapeDtypeStruct(state[0].shape, BF),
        jax.ShapeDtypeStruct(state[0].shape, BF),
        jax.ShapeDtypeStruct((6 * width, channels), BF),
        jax.ShapeDtypeStruct((6 * width, channels), BF),
        *[jax.ShapeDtypeStruct((12 * width, channels), BF)] * (1 + len(older)),
    )
    return pl.pallas_call(
        functools.partial(section_kernel, width, high, parity),
        out_shape=shapes,
        in_specs=[VM] * 4 + [ANY] * 10 + [VM] * len(older),
        out_specs=[VM] * len(shapes),
        scratch_shapes=[
            pltpu.VMEM((9 * channels, channels), BF),
            pltpu.VMEM((9 * channels, channels), BF),
            pltpu.SemaphoreType.DMA,
            pltpu.SemaphoreType.DMA,
        ],
        compiler_params=pltpu.CompilerParams(vmem_limit_bytes=GRANT),
        cost_estimate=pl.CostEstimate(
            flops=48 * 9 * width * channels * channels, bytes_accessed=4 << 20, transcendentals=0
        ),
        name="section_step",
    )(*state, *got, *weights, *older)


def prepare_kernel(
    width, top_hbm, low_hbm, own_ref, senda_ref, sendb_ref, early_ref, pick_ref, top_ref, low_ref, sem
):
    row = lax.axis_index("rows")
    even = row % 2 == 0
    core = lax.axis_index("sec") % 2
    quarter = quarter_of(row) ^ 1
    copies = [
        pltpu.make_async_copy(own_ref.at[1 - core, quarter], early_ref, sem.at[0]),
        pltpu.make_async_copy(own_ref.at[core, quarter], pick_ref, sem.at[1]),
        pltpu.make_async_copy(top_hbm, top_ref, sem.at[2]),
        pltpu.make_async_copy(low_hbm, low_ref, sem.at[3]),
    ]
    for copy in copies:
        copy.start()
    for copy in copies[2:]:
        copy.wait()
    w = width
    for ref, low in ((senda_ref, even), (sendb_ref, jnp.logical_not(even))):
        ref[: 2 * w] = top_ref[0]
        ref[2 * w : 4 * w] = low_ref[1]
        for place, both_ref in ((4, top_ref.at[1]), (5, low_ref.at[0])):
            both = both_ref[...].astype(F32)
            ref[place * w : (place + 1) * w] = jnp.where(low, both[w:], both[:w]).astype(BF)
    for copy in copies[:2]:
        copy.wait()


def prepare(state, halves):
    _, pixels, channels = state[0].shape
    width = pixels // 2
    edge = jax.ShapeDtypeStruct((6 * width, channels), BF)
    piece = jax.ShapeDtypeStruct(halves.shape[2:], BF)
    return pl.pallas_call(
        functools.partial(prepare_kernel, width),
        out_shape=(edge, edge, piece, piece),
        in_specs=[pl.BlockSpec(memory_space=pltpu.HBM)] * 3,
        out_specs=[VM] * 4,
        scratch_shapes=[
            pltpu.VMEM(state[0].shape, BF),
            pltpu.VMEM(state[0].shape, BF),
            pltpu.SemaphoreType.DMA((4,)),
        ],
        compiler_params=pltpu.CompilerParams(vmem_limit_bytes=GRANT),
        name="prepare",
    )(*state, halves)


def choose_kernel(early_ref, pick_ref, odd_ref, even_ref):
    core = lax.axis_index("sec") % 2

    @pl.when(core == 0)
    def _():
        odd_ref[...] = early_ref[...]
        even_ref[...] = pick_ref[...]

    @pl.when(core == 1)
    def _():
        odd_ref[...] = pick_ref[...]
        even_ref[...] = early_ref[...]


def choose(early, pick):
    return pl.pallas_call(
        choose_kernel,
        out_shape=(jax.ShapeDtypeStruct(early.shape, BF),) * 2,
        in_specs=[VM, VM],
        out_specs=[VM, VM],
        compiler_params=pltpu.CompilerParams(vmem_limit_bytes=GRANT),
        name="choose",
    )(early, pick)


def grads_kernel(width, sources, *refs):
    ins, (keepa, senda, keepb, sendb, a0, a1, a2, a3, acc_ref, sem) = refs[:8], refs[8:]
    w = width
    channels = a0.shape[-1]
    sec = lax.axis_index("sec")
    for section, picks in sources.items():

        @pl.when(sec == section)
        def _(picks=picks):
            for out, pick in zip((a0, a1, a2, a3), picks):
                pltpu.make_async_copy(ins[pick], out, sem).start()

    for out in (a0, a1, a2, a3):
        pltpu.make_async_copy(ins[0], out, sem).wait()
    row = lax.axis_index("rows")
    ylow, x = row // (NX * NZ) % 2, row // NZ % NX
    for kernel, (act_at, cot_at) in enumerate(((6, 10), (0, 4))):
        shifts = []
        for ref in (a0, a1, a2, a3):
            shifts.append(col_shifts(ref[act_at * w : (act_at + 4) * w].astype(F32), w))
        cot = jnp.concatenate([ref[cot_at * w : (cot_at + 2) * w] for ref in (a0, a1, a2, a3)], 0)
        for a in range(3):
            for b in range(3):
                act = jnp.concatenate([s[b][a * w : (a + 2) * w] for s in shifts], 0)
                at = ((kernel * 3 + a) * 3 + b) * channels
                acc_ref[at : at + channels] = lax.dot_general(
                    act, cot, (((0,), (0,)), ((), ())), preferred_element_type=F32
                )
    size = 18 * channels // 8
    cols = channels // 2

    def region(yhigh, ylow, x):
        return pl.ds(pl.multiple_of(((yhigh * 2 + ylow) * 2 + x) * size, 8), size)

    for i in range(2):
        for j in range(2):
            keepa[i, j] = acc_ref[region(i, j, x), :cols]
            senda[i, j] = acc_ref[region(i, j, 1 - x), :cols].astype(BF)
            keepb[i, j] = acc_ref[region(i, ylow, j), cols:]
            sendb[i, j] = acc_ref[region(i, 1 - ylow, j), cols:].astype(BF)


def section_grads(arrays, sources, width):
    channels = arrays[0].shape[-1]
    shape = (2, 2, 18 * channels // 8, channels // 2)
    return pl.pallas_call(
        functools.partial(grads_kernel, width, sources),
        out_shape=tuple(jax.ShapeDtypeStruct(shape, kind) for kind in (F32, BF, F32, BF)),
        in_specs=[ANY] * 8,
        out_specs=[VM] * 4,
        scratch_shapes=[pltpu.VMEM(arrays[0].shape, BF)] * 4
        + [pltpu.VMEM((18 * channels, channels), F32), pltpu.SemaphoreType.DMA],
        compiler_params=pltpu.CompilerParams(vmem_limit_bytes=GRANT),
        name="section_grads",
    )(*arrays)


def halve_kernel(keepa, gota, keepb, gotb, keepa2, senda2, keepb2, sendb2):
    row = lax.axis_index("rows")
    ylow, x = row // (NX * NZ) % 2, row // NZ % NX
    for keep, got, keep2, send2, bit in ((keepa, gota, keepa2, senda2, ylow), (keepb, gotb, keepb2, sendb2, x)):
        for i in range(2):
            keep2[i] = keep[i, bit] + got[i, bit].astype(F32)
            send2[i] = (keep[i, 1 - bit] + got[i, 1 - bit].astype(F32)).astype(BF)


def halve(keepa, gota, keepb, gotb):
    shape = keepa.shape[:1] + keepa.shape[2:]
    return pl.pallas_call(
        halve_kernel,
        out_shape=tuple(jax.ShapeDtypeStruct(shape, kind) for kind in (F32, BF, F32, BF)),
        in_specs=[VM] * 4,
        out_specs=[VM] * 4,
        compiler_params=pltpu.CompilerParams(vmem_limit_bytes=GRANT),
        name="halve_terms",
    )(keepa, gota, keepb, gotb)


def join_kernel(keepa, gota, keepb, gotb, out):
    cols = keepa.shape[-1]
    out[:, :, :cols] = (keepa[...] + gota[...].astype(F32)).astype(BF)
    out[:, :, cols:] = (keepb[...] + gotb[...].astype(F32)).astype(BF)


def join(keepa, gota, keepb, gotb):
    shape = keepa.shape[:-1] + (2 * keepa.shape[-1],)
    return pl.pallas_call(
        join_kernel,
        out_shape=jax.ShapeDtypeStruct(shape, BF),
        in_specs=[VM] * 4,
        out_specs=VM,
        compiler_params=pltpu.CompilerParams(vmem_limit_bytes=GRANT),
        name="join_terms",
    )(keepa, gota, keepb, gotb)


def local(streams, cotangents, weights):
    rows = lax.axis_size("rows")
    ny = rows // (NX * NZ)
    crops, _, height_dev, width, channels = streams.shape
    sec = lax.axis_index("sec")
    scale = float(4 * height_dev * rows * width) ** -0.5

    cross_pairs = []
    for s in range(4):
        for r in range(rows):
            cross_pairs.append((s * rows + r, (s ^ 2) * rows + (r ^ NZ)))
    pairs_a = [(r, r ^ 1) for r in range(rows)]
    pairs_b = [p for r in range(1, rows - 1, 2) for p in ((r, r + 1), (r + 1, r))]

    def core_swap(value):
        return lax.ppermute(value, "sec", [(s, s ^ 1) for s in range(4)])

    def cross(value):
        return lax.ppermute(value, ("sec", "rows"), cross_pairs)

    def flip(value, bit):
        return lax.ppermute(value, "rows", [(r, r ^ bit) for r in range(rows)])

    def hand_over(value, pairs):
        far = [
            (a * rows + r, b * rows + (r ^ NZ if (a ^ b) & 2 else r)) for a, b in pairs for r in range(rows)
        ]
        return lax.ppermute(value, ("sec", "rows"), far)

    def halo(sends):
        return lax.ppermute(sends[0], "rows", pairs_a), lax.ppermute(sends[1], "rows", pairs_b)

    own = weights[0, 0].reshape(2, 9 * channels, channels)
    state = [part.reshape(2, height_dev * width, channels) for part in (streams, cotangents)]
    *sends, early, pick = prepare(state, own.reshape(2, 4, 9 * channels // 4, channels))
    odd, even = choose(core_swap(early), pick)
    odd = cross(odd)
    got = halo(sends)
    swapped = core_swap(own)
    odd, swapped, even, *got = barrier((odd, swapped, even, *got))
    bits = (NZ, NX * NZ, 1)
    odds = [odd] + [flip(odd, bit) for bit in bits]
    even = cross(even)
    even, *odds = barrier((even, *odds))
    evens = [even] + [flip(even, bit) for bit in bits]
    far = {1: (*odds, *map(core_swap, odds))}
    acts = {}
    moved = {}
    for section in (3, 2, 1, 0):
        parity = section % 2
        older = [acts[section + 2]] if section < 2 else []
        top, low, senda, sendb, *new = section_step(
            section // 2, parity, state, got, (own, swapped) + far[parity], older
        )
        state = [top, low]
        acts[section] = new[0]
        if section:
            got = halo((senda, sendb))
        if section == 3:
            state[0], *evens = barrier((state[0], *evens))
            far[0] = (*evens, *map(core_swap, evens))
        if section < 2:
            here, there = new
            to = section
            moved[section] = (
                hand_over(here, [(1 - to, to), (3 - to, 2 + to)]),
                hand_over(there, [(to, 2 + to), (2 + to, to)]),
                hand_over(there, [(1 - to, 2 + to), (3 - to, to)]),
            )

    arrays = [acts[0], *moved[0], acts[1], *moved[1]]
    sources = {s: tuple(range(4 * (s % 2), 4 + 4 * (s % 2))) for s in range(4)}
    keepa, senda, keepb, sendb = section_grads(arrays, sources, width)
    gota, gotb = flip(senda, NZ), flip(sendb, NX * NZ)
    keepa, senda, keepb, sendb = halve(keepa, gota, keepb, gotb)
    gota, gotb = flip(senda, NX * NZ), flip(sendb, NZ)
    total = join(keepa, gota, keepb, gotb).reshape(2 * NZ, -1, channels)
    groups = [
        [((yhigh * 2 + ylow) * NX + x) * NZ + z for yhigh in range(ny // 2) for z in range(NZ)]
        for ylow in range(2)
        for x in range(NX)
    ]
    parts = lax.all_to_all(total, "rows", 0, 0, axis_index_groups=groups)
    shard = jnp.sum(parts.astype(F32), 0) * scale
    result = [part.reshape(1, 2, height_dev, width, channels) for part in state]
    return *result, shard[None]


def solution(mesh):
    placed = (
        P("sec", None, "rows", None, None),
        P("sec", None, "rows", None, None),
        P("sec", None, None, None, None, None, None),
    )
    return jax.shard_map(
        local,
        mesh=mesh,
        in_specs=placed,
        out_specs=(
            P("sec", None, "rows", None, None),
            P("sec", None, "rows", None, None),
            P("sec", "rows", None),
        ),
        check_vma=False,
    )
```
